32 devices in a mesh: mom: 2 (over x), en: 16 (over z, y, core).
Axes of the slice: x: 2, y: 2, z: 4, core: 2. Of those that a mesh axis runs over, the one named last changes fastest.
Arguments:
- green: bfloat16 [8, 128, 8, 2, 256], P('mom', 'en'), may hold values from -6 to 6
- phonon: bfloat16 [8, 2, 2, 9, 2, 8], replicated, may hold values from -0.75 to 0.75
- coupling: bfloat16 [3, 4, 16, 16], replicated, may hold values from -0.875 to 0.875
- neighbours: int32 [4, 2], replicated, may hold values from 0 to 3
- momentum_table: int32 [8, 8], P('mom'), may hold values from 0 to 7, as said below
- shifts: int32 [2], replicated, may hold values from 1 to 8
Outputs:
- self_energy: float32 [8, 128, 8, 2, 256], P('mom', 'en')
The draws below stay inside these ranges and needn't reach their ends.
Inputs may be any that keep to these rules, and one draw needn't show every extreme that they name: Each momentum point has a coordinate modulo 8, all distinct; momentum_table[k, k2] depends only on the coordinate of point k minus that of point k2 modulo 8, distinct differences giving distinct indices; each row and each column is a permutation.
All inputs are finite; a program needn't handle non-finite values.
Results may differ from the reference program's by a relative error of at most 0.0041.
Values may be sent and summed in bfloat16 or wider, within the bound.
A program may use at most 128 MiB of HBM per device.

```python
import jax
import jax.numpy as jnp
from jax import lax

ORB = 16
NBR = 2
ATOMS = 4
E_DEV = 8
NW = 2
PAIRS = 8
NK = 8
NE = 128


def draw_momentum_table(key, part):
    order = jax.random.permutation(jax.random.fold_in(key, 11), NK).astype(jnp.int32)
    relabel = jax.random.permutation(jax.random.fold_in(key, 13), NK).astype(jnp.int32)
    difference = ((order[:, None] - order[None, :]) % NK).astype(jnp.int32)
    return relabel[difference].astype(jnp.int32)


def draw_shifts(key, part):
    first = jax.random.fold_in(key, 23)
    second = jax.random.fold_in(key, 29)
    values = jax.random.randint(first, (NW,), 1, E_DEV + 1).astype(jnp.int32)
    chosen = jax.random.randint(second, (), 0, NW).astype(jnp.int32)
    return jnp.where(jnp.arange(NW) == chosen, E_DEV, values).astype(jnp.int32)


def with_ends(values, stream_key, low, high):
    longest = values.shape.index(max(values.shape))
    spots = []
    for shift in (0, 1):
        where = [jax.random.randint(jax.random.fold_in(stream_key, axis), (), 0, length) for axis, length in enumerate(values.shape)]
        where[longest] = (where[longest] + shift) % values.shape[longest]
        spots.append(tuple(where))
    return values.at[spots[0]].set(low).at[spots[1]].set(high)


def shard_levels(stream_key, dims, shards, low, largest):
    def one(dim, shards_of):
        steps = jax.random.uniform(jax.random.fold_in(jax.random.fold_in(stream_key, 6), dim), (shards_of,), jnp.float32, low / len(shards), largest / len(shards))
        return jnp.repeat(jnp.exp(steps), dims[dim] // shards_of).reshape((-1,) + (1,) * (len(dims) - dim - 1))

    gain = one(*shards[0])
    for cut in shards[1:]:
        gain = gain * one(*cut)
    return gain


def scatter_about(own_key, shape, spread, most, shards=(), kind=jnp.bfloat16):
    entries = jax.random.normal(own_key, shape, jnp.float32) * spread
    if len(shards) > 0:
        entries = shard_levels(own_key, shape, shards, -0.22, 0.18) * entries
    return jnp.clip(entries, min=-most, max=most).astype(kind)


def setup_inputs(seed: int = 0) -> dict:
    splits = jax.random.split(jax.random.key(seed), 7)
    return {
        "green": scatter_about(splits[0], (NK, NE, PAIRS, 2, ORB * ORB), 1.0, 6.0, ((0, 2), (1, 16))),
        "phonon": scatter_about(splits[1], (NK, NW, 2, 9, 2, PAIRS), (4 * NK * NW) ** -0.5, 0.75),
        "coupling": scatter_about(splits[2], (3, ATOMS, ORB, ORB), 48 ** -0.5, 0.875),
        "neighbours": with_ends(jax.random.randint(splits[3], (ATOMS, NBR), 0, ATOMS), jax.random.fold_in(splits[3], 1), 0, ATOMS - 1).astype(jnp.int32),
        "momentum_table": draw_momentum_table(jax.random.fold_in(splits[6], 71), 0),
        "shifts": draw_shifts(jax.random.fold_in(splits[6], 71), 0),
    }


def narrow_round(values):
    return lax.optimization_barrier(values.astype(jnp.bfloat16)).astype(jnp.float32)


def reference(green, phonon, coupling, neighbours, momentum_table, shifts):
    count_energy = green.shape[1]
    count_pairs = green.shape[2]
    padded = jnp.pad(green.astype(jnp.float32), ((0, 0), (E_DEV, E_DEV), (0, 0), (0, 0), (0, 0)))
    atom_ids = (jnp.arange(count_pairs) // NBR).astype(jnp.int32)
    left = jnp.take(coupling, atom_ids, axis=1).astype(jnp.float32)
    right = jnp.take(coupling, neighbours.reshape(-1).astype(jnp.int32), axis=1).astype(jnp.float32)
    coef_all = phonon.astype(jnp.float32)

    def one_momentum(table_row):
        coef = jnp.take(coef_all, table_row.astype(jnp.int32), axis=0)

        def add_frequency(summed, freq):
            for sense in range(2):
                if sense == 0:
                    start = (E_DEV - shifts[freq]).astype(jnp.int32)
                else:
                    start = (E_DEV + shifts[freq]).astype(jnp.int32)
                window = lax.dynamic_slice_in_dim(padded, start, count_energy, 1)
                coef_re = coef[:, freq, sense, :, 0, :]
                coef_im = coef[:, freq, sense, :, 1, :]
                part_re = jnp.einsum("bjp,bepq->jpeq", coef_re, window[:, :, :, 0]) - jnp.einsum("bjp,bepq->jpeq", coef_im, window[:, :, :, 1])
                part_im = jnp.einsum("bjp,bepq->jpeq", coef_im, window[:, :, :, 0]) + jnp.einsum("bjp,bepq->jpeq", coef_re, window[:, :, :, 1])
                summed = summed + jnp.stack([part_re, part_im], axis=2)
            return summed, None

        start_sum = jnp.zeros((9, count_pairs, 2, count_energy, ORB * ORB), jnp.float32)
        fsum, _ = lax.scan(add_frequency, start_sum, jnp.arange(phonon.shape[1]))
        fsum = narrow_round(fsum).reshape(3, 3, count_pairs, 2, count_energy, ORB, ORB)
        half = narrow_round(jnp.einsum("ijpceon,jpmn->ipceom", fsum, right))
        result = jnp.einsum("iplo,ipceom->epclm", left, half)
        return result.reshape(count_energy, count_pairs, 2, ORB * ORB)

    return lax.map(one_momentum, momentum_table)
```

```python
import functools

import jax
import jax.numpy as jnp
from jax import lax
from jax.experimental import pallas as pl
from jax.experimental.pallas import tpu as pltpu
from jax.sharding import PartitionSpec as P

ORB = 16
MESH = pl.DeviceIdType.MESH
BF = jnp.bfloat16
F32 = jnp.float32


def dot(a, b):
    return jnp.dot(a, b, preferred_element_type=F32)


def dot_t(a, b):
    return lax.dot_general(a, b, (((1,), (1,)), ((), ())), preferred_element_type=F32)


def iota(shape, dim):
    return lax.broadcasted_iota(jnp.int32, shape, dim)


def kernel(moms, slabs, neigh_any, shift_any, table_any, green_ref, phonon_any, coup_any, out_ref,
           neigh_ref, shift_ref, table_ref, phonon_ref, coup_ref, small_sem, coef, right, left, part, fsum, own_sem, send_mom, recv_mom, send_halo, recv_halo, send_relay, *bufs):
    mom = lax.axis_index("mom")
    en = lax.axis_index("en")
    count_k, count_e = green_ref.shape[0], green_ref.shape[1]
    pairs = green_ref.shape[2]
    rows = 2 * pairs
    kinds, atoms = coup_ref.shape[0], coup_ref.shape[1]
    has_prev = en > 0
    has_next = en < slabs - 1

    own = pltpu.make_async_copy(green_ref, bufs[0].at[:, pl.ds(count_e, count_e)], own_sem)

    barrier = pltpu.get_barrier_semaphore()

    def mom_peer(r):
        return {"mom": lax.rem(mom + moms - r, moms)}

    for r in range(1, moms):
        pl.semaphore_signal(barrier, inc=1, device_id=mom_peer(r), device_id_type=MESH)

    @pl.when(has_prev)
    def _():
        pl.semaphore_signal(barrier, inc=1, device_id={"en": en - 1}, device_id_type=MESH)

    @pl.when(has_next)
    def _():
        pl.semaphore_signal(barrier, inc=1, device_id={"en": en + 1}, device_id_type=MESH)

    pl.semaphore_wait(
        barrier, moms - 1 + jnp.where(has_prev, 1, 0) + jnp.where(has_next, 1, 0)
    )

    def mom_copy(r, k):
        return pltpu.make_async_remote_copy(
            src_ref=green_ref.at[k],
            dst_ref=bufs[r].at[k, pl.ds(count_e, count_e)],
            send_sem=send_mom.at[r, k],
            recv_sem=recv_mom.at[r, k],
            device_id=mom_peer(r),
            device_id_type=MESH,
        )

    def halo_copy(d, r, k):
        src = green_ref.at[k] if r == 0 else bufs[r].at[k, pl.ds(count_e, count_e)]
        return pltpu.make_async_remote_copy(
            src_ref=src,
            dst_ref=bufs[r].at[k, pl.ds(2 * count_e * d, count_e)],
            send_sem=send_halo.at[d, r, k],
            recv_sem=recv_halo.at[d, r, k],
            device_id={"en": en + 1 - 2 * d},
            device_id_type=MESH,
        )

    small = [
        pltpu.make_async_copy(src, dst, small_sem.at[i])
        for i, (src, dst) in enumerate([
            (phonon_any, phonon_ref), (table_any, table_ref), (coup_any, coup_ref),
            (neigh_any, neigh_ref), (shift_any, shift_ref),
        ])
    ]

    near = en % 2
    far = 1 - near
    has_far = jnp.where(near == 0, has_prev, has_next)
    split = count_k // 2

    def relay_copy(r, k):
        place = pl.ds(2 * count_e * near, count_e)
        return pltpu.make_async_remote_copy(
            src_ref=bufs[0].at[k, place],
            dst_ref=bufs[r].at[k, place],
            send_sem=send_relay.at[r, k],
            recv_sem=recv_halo.at[near, r, k],
            device_id=mom_peer(r),
            device_id_type=MESH,
        )

    def when_sent(r, k, act):
        if r == 0 or k < split:
            @pl.when(has_next)
            def _():
                act(halo_copy(0, r, k))

            @pl.when(has_prev)
            def _():
                act(halo_copy(1, r, k))
        else:
            act(halo_copy(near, r, k))

    start = lambda copy: copy.start()
    for k in range(count_k):
        for r in range(1, moms):
            mom_copy(r, k).start()
        when_sent(0, (k + split) % count_k, start)
    for copy in small:
        copy.start()
    own.start()

    @pl.when(jnp.logical_not(has_prev))
    def _():
        for r in range(moms):
            for k in range(count_k):
                bufs[r][k, pl.ds(0, count_e)] = jnp.zeros((count_e, pairs, 2, ORB * ORB), BF)

    @pl.when(jnp.logical_not(has_next))
    def _():
        for r in range(moms):
            for k in range(count_k):
                bufs[r][k, pl.ds(2 * count_e, count_e)] = jnp.zeros((count_e, pairs, 2, ORB * ORB), BF)

    q = ORB * ORB
    low = jnp.where(iota((q, ORB), 0) % ORB == iota((q, ORB), 1), 1.0, 0.0).astype(BF)
    high = jnp.where(iota((q, ORB), 0) // ORB == iota((q, ORB), 1), 1.0, 0.0).astype(BF)
    low_t = jnp.where(iota((ORB, q), 1) % ORB == iota((ORB, q), 0), 1.0, 0.0).astype(BF)
    high_t = jnp.where(iota((ORB, q), 1) // ORB == iota((ORB, q), 0), 1.0, 0.0).astype(BF)
    same_high = iota((q, q), 0) // ORB == iota((q, q), 1) // ORB
    same_low = iota((q, q), 0) % ORB == iota((q, q), 1) % ORB

    def build(index):
        i, a = index
        block = coup_ref[i, a]
        wide = dot(dot_t(low, block).astype(BF), low_t)
        right[a, i] = jnp.where(same_high, wide, 0.0).astype(BF)
        tall = dot(dot_t(high, block).astype(BF), high_t)
        left[a, i] = jnp.where(same_low, tall, 0.0).astype(BF)

    for copy in small:
        copy.wait()

    count_b, spots, ijs = phonon_ref.shape
    senses = spots // (2 * pairs)
    height, width = ijs * 2 * count_k, senses * count_k * rows
    unit = iota((height, ijs), 0) // (2 * count_k)
    unit = (unit % kinds) * kinds + unit // kinds
    pick = jnp.where(unit == iota((height, ijs), 1), 1.0, 0.0).astype(BF)
    col = iota((spots, width), 1)
    spot = iota((spots, width), 0)
    base = (col // (count_k * rows)) * (2 * pairs) + (col % rows) // 2
    take_re = jnp.where(base == spot, 1.0, 0.0).astype(BF)
    take_im = jnp.where(base + pairs == spot, 1.0, 0.0).astype(BF)
    across = jnp.concatenate(
        [dot_t(pick, phonon_ref[b]).astype(BF) for b in range(count_b)], axis=0
    )
    row_part = iota((2 * count_k, width), 0) % 2
    col_part = iota((2 * count_k, width), 1) % 2
    row_k = iota((2 * count_k, width), 0) // 2
    col_k = (iota((2 * count_k, width), 1) // rows) % count_k
    sign = jnp.where(row_part < col_part, -1.0, 1.0)
    real = dot(across, take_re).reshape(count_b, ijs, 2 * count_k, width)
    imag = dot(across, take_im).reshape(count_b, ijs, 2 * count_k, width) * sign
    table_b = jnp.where(row_part == col_part, real, imag)
    pair_of = (iota((pairs, 1, width), 2) % rows) // 2 == iota((pairs, 1, width), 0)

    def coefficients(r):
        first = lax.rem(mom + r, moms) * count_k
        index = jnp.zeros((2 * count_k, width), jnp.int32)
        for k in range(count_k):
            for other in range(count_k):
                here = jnp.logical_and(row_k == k, col_k == other)
                index = jnp.where(here, table_ref[k, first + other], index)
        dense = jnp.zeros((ijs, 2 * count_k, width), F32)
        for b in range(count_b):
            dense = jnp.where(index == b, table_b[b], dense)
        dense = dense.reshape(1, height, width)
        coef[r] = jnp.where(pair_of, dense, 0.0).reshape(pairs * height, width).astype(BF)

    freqs = shift_ref.shape[0]
    starts = []
    for w in range(freqs):
        starts += [count_e - shift_ref[w], count_e + shift_ref[w]]

    def term(r, e):
        window = jnp.concatenate(
            [bufs[r][k, e + start].reshape(rows, q) for start in starts for k in range(count_k)], axis=0
        )
        return dot(coef[r], window)

    def wait_halo(r):
        for k in range(count_k):
            if r == 0 and k >= split:
                halo_copy(far, r, k).wait_recv()
            else:
                @pl.when(has_prev)
                def _():
                    halo_copy(0, r, k).wait_recv()

                @pl.when(has_next)
                def _():
                    halo_copy(1, r, k).wait_recv()

    todo = [(i, a) for i in range(kinds) for a in range(atoms)]
    for r in range(moms):
        coefficients(r)
    share = -(-len(todo) // count_k)
    for k in range(count_k):
        for r in range(1, moms):
            mom_copy(r, k).wait_recv()
            when_sent(r, k, start)
        for index in todo[k * share:k * share + share // 2]:
            build(index)
        late = k + split
        if late < count_k:
            @pl.when(has_far)
            def _():
                halo_copy(near, 0, late).wait_recv()
                for r in range(1, moms):
                    relay_copy(r, late).start()
        for index in todo[k * share + share // 2:(k + 1) * share]:
            build(index)
    own.wait()
    for r in range(moms - 1):
        wait_halo(r)

        def add(e, carry):
            part[e] = term(r, e) if r == 0 else part[e] + term(r, e)
            return carry

        lax.fori_loop(0, count_e, add, 0, unroll=4)
    wait_halo(moms - 1)

    def summed(e):
        return (part[e] + term(moms - 1, e)).reshape(-1, 2 * count_k, q) if moms > 1 else term(0, e).reshape(-1, 2 * count_k, q)

    def two(step, carry):
        both = jnp.concatenate([summed(2 * step), summed(2 * step + 1)], axis=1)
        fsum[:, pl.ds(pl.multiple_of(step * 4 * count_k, 4 * count_k), 4 * count_k), :] = both.astype(BF)
        return carry

    lax.fori_loop(0, count_e // 2, two, 0, unroll=True)

    units = kinds * kinds
    per_atom = pairs // atoms
    size = count_e * count_k * 2

    for a in range(atoms):
        halves = []
        for n in range(per_atom):
            p = a * per_atom + n
            nb = neigh_ref[n, a]
            half = None
            for j in range(kinds):
                rows_j = fsum[pl.ds(p * units + j * kinds, kinds)].reshape(-1, q)
                piece = dot(rows_j, right[nb, j])
                half = piece if half is None else half + piece
            halves.append(half.astype(BF).reshape(kinds, size, q))
        result = None
        for i in range(kinds):
            both = jnp.concatenate([half[i] for half in halves], axis=0)
            piece = dot(both, left[a, i])
            result = piece if result is None else result + piece
        for n in range(per_atom):
            for e in range(count_e):
                for k in range(count_k):
                    row = n * size + 2 * (e * count_k + k)
                    out_ref[k, e, a * per_atom + n] = result[row:row + 2]

    for k in range(count_k):
        for r in range(moms):
            when_sent(r, k, lambda copy: copy.wait_send())
            if r > 0:
                mom_copy(r, k).wait_send()
                if k >= split:
                    @pl.when(has_far)
                    def _():
                        relay_copy(r, k).wait_send()


def shards(green, phonon, coupling, neighbours, momentum_table, shifts):
    moms, slabs = lax.axis_size("mom"), lax.axis_size("en")
    count_k, count_e, pairs = green.shape[:3]
    q = green.shape[4]
    kinds, atoms = coupling.shape[:2]
    ijs = phonon.shape[3]
    count_b = phonon.shape[0]
    spread = phonon.transpose(0, 1, 2, 4, 5, 3).reshape(count_b, -1, ijs)
    height, width = ijs * 2 * count_k, phonon.shape[1] * 2 * count_k * 2 * pairs
    out = pl.pallas_call(
        functools.partial(kernel, moms, slabs),
        out_shape=pltpu.VMEM(green.shape, F32),
        in_specs=[pl.BlockSpec(memory_space=pltpu.HBM)] * 6,
        out_specs=pl.BlockSpec(memory_space=pltpu.VMEM),
        scratch_shapes=[
            pltpu.SMEM(neighbours.T.shape, jnp.int32),
            pltpu.SMEM(shifts.shape, jnp.int32),
            pltpu.SMEM(momentum_table.shape, jnp.int32),
            pltpu.VMEM(spread.shape, BF),
            pltpu.VMEM(coupling.shape, BF),
            pltpu.SemaphoreType.DMA((5,)),
            pltpu.VMEM((moms, pairs * height, width), BF),
            pltpu.VMEM((atoms, kinds, q, q), BF),
            pltpu.VMEM((atoms, kinds, q, q), BF),
            pltpu.VMEM((count_e, pairs * height, q), F32),
            pltpu.VMEM((pairs * kinds * kinds, count_e * count_k * 2, q), BF),
            pltpu.SemaphoreType.DMA,
            pltpu.SemaphoreType.DMA((moms, count_k)),
            pltpu.SemaphoreType.DMA((moms, count_k)),
            pltpu.SemaphoreType.DMA((2, moms, count_k)),
            pltpu.SemaphoreType.DMA((2, moms, count_k)),
            pltpu.SemaphoreType.DMA((moms, count_k)),
        ] + [pltpu.VMEM((count_k, 3 * count_e, pairs, 2, q), BF)] * moms,
        compiler_params=pltpu.CompilerParams(collective_id=0, has_side_effects=True, vmem_limit_bytes=32 * 1024 * 1024),
    )(*[pltpu.with_memory_space_constraint(x, pltpu.HBM) for x in (neighbours.T, shifts, momentum_table, green, spread, coupling)])
    return out


def solution(mesh):
    return jax.shard_map(
        shards,
        mesh=mesh,
        in_specs=(P("mom", "en", None, None, None), P(), P(), P(), P("mom", None), P()),
        out_specs=P("mom", "en", None, None, None),
        check_vma=False,
    )
```

```python
import functools

import jax
import jax.numpy as jnp
from jax import lax
from jax.experimental import pallas as pl
from jax.experimental.pallas import tpu as pltpu
from jax.sharding import PartitionSpec as P

ORB = 16
MESH = pl.DeviceIdType.MESH
BF = jnp.bfloat16
F32 = jnp.float32


def dot(a, b):
    return jnp.dot(a, b, preferred_element_type=F32)


def dot_first(a, b):
    return lax.dot_general(a, b, (((0,), (0,)), ((), ())), preferred_element_type=F32)


def iota(shape, dim):
    return lax.broadcasted_iota(jnp.int32, shape, dim)


def one_hot(mask):
    return jnp.where(mask, 1.0, 0.0).astype(BF)


def kernel(moms, slabs, neigh_any, shift_any, table_any, green_ref, phonon_any, coup_any, out_ref,
           neigh_ref, shift_ref, table_ref, phonon_ref, coup_ref, right, left, coef_own, coef_side,
           rot, sums, half, small_sem, own_sem, send_mom, recv_mom, send_halo, recv_halo, send_relay, *bufs):
    mom = lax.axis_index("mom")
    en = lax.axis_index("en")
    count_k, count_e, pairs = green_ref.shape[0], green_ref.shape[1], green_ref.shape[2]
    q = green_ref.shape[4]
    kinds, atoms = coup_ref.shape[0], coup_ref.shape[1]
    per_atom = pairs // atoms
    freqs = shift_ref.shape[0]
    block = per_atom * count_k * 2
    unit = kinds * block
    side = freqs * unit
    width = 2 * side
    tile = right.shape[1]
    has_prev = en > 0
    has_next = en < slabs - 1

    own = pltpu.make_async_copy(green_ref, bufs[0].at[:, pl.ds(count_e, count_e)], own_sem)

    barrier = pltpu.get_barrier_semaphore()

    def mom_peer(r):
        return {"mom": lax.rem(mom + moms - r, moms)}

    for r in range(1, moms):
        pl.semaphore_signal(barrier, inc=1, device_id=mom_peer(r), device_id_type=MESH)

    @pl.when(has_prev)
    def _():
        pl.semaphore_signal(barrier, inc=1, device_id={"en": en - 1}, device_id_type=MESH)

    @pl.when(has_next)
    def _():
        pl.semaphore_signal(barrier, inc=1, device_id={"en": en + 1}, device_id_type=MESH)

    pl.semaphore_wait(
        barrier, moms - 1 + jnp.where(has_prev, 1, 0) + jnp.where(has_next, 1, 0)
    )

    def mom_copy(r, k):
        return pltpu.make_async_remote_copy(
            src_ref=green_ref.at[k],
            dst_ref=bufs[r].at[k, pl.ds(count_e, count_e)],
            send_sem=send_mom.at[r, k],
            recv_sem=recv_mom.at[r, k],
            device_id=mom_peer(r),
            device_id_type=MESH,
        )

    def halo_copy(d, r, k):
        src = green_ref.at[k] if r == 0 else bufs[r].at[k, pl.ds(count_e, count_e)]
        return pltpu.make_async_remote_copy(
            src_ref=src,
            dst_ref=bufs[r].at[k, pl.ds(2 * count_e * d, count_e)],
            send_sem=send_halo.at[d, r, k],
            recv_sem=recv_halo.at[d, r, k],
            device_id={"en": en + 1 - 2 * d},
            device_id_type=MESH,
        )

    small = [
        pltpu.make_async_copy(src, dst, small_sem.at[i])
        for i, (src, dst) in enumerate([
            (coup_any, coup_ref), (phonon_any, phonon_ref), (table_any, table_ref),
            (neigh_any, neigh_ref), (shift_any, shift_ref),
        ])
    ]

    near = en % 2
    far = 1 - near
    has_far = jnp.where(near == 0, has_prev, has_next)
    split = count_k // 2

    def relay_copy(r, k):
        place = pl.ds(2 * count_e * near, count_e)
        return pltpu.make_async_remote_copy(
            src_ref=bufs[0].at[k, place],
            dst_ref=bufs[r].at[k, place],
            send_sem=send_relay.at[r, k],
            recv_sem=recv_halo.at[near, r, k],
            device_id=mom_peer(r),
            device_id_type=MESH,
        )

    def when_sent(r, k, act):
        if r == 0 or k < split:
            @pl.when(has_next)
            def _():
                act(halo_copy(0, r, k))

            @pl.when(has_prev)
            def _():
                act(halo_copy(1, r, k))
        else:
            act(halo_copy(near, r, k))

    start = lambda copy: copy.start()
    for k in range(count_k):
        for r in range(1, moms):
            mom_copy(r, k).start()
        when_sent(0, (k + split) % count_k, start)
    for copy in small:
        copy.start()
    own.start()

    @pl.when(jnp.logical_not(has_prev))
    def _():
        for r in range(moms):
            for k in range(count_k):
                bufs[r][k, pl.ds(0, count_e)] = jnp.zeros((count_e, pairs, 2, q), BF)

    @pl.when(jnp.logical_not(has_next))
    def _():
        for r in range(moms):
            for k in range(count_k):
                bufs[r][k, pl.ds(2 * count_e, count_e)] = jnp.zeros((count_e, pairs, 2, q), BF)

    lane = iota((ORB, tile + q), 1)
    spread = one_hot(jnp.where(lane < tile, lane % ORB, (lane - tile) // ORB) == iota((ORB, tile + q), 0))
    same_high = iota((tile, tile), 0) // ORB == iota((tile, tile), 1) // ORB
    same_low = iota((q, q), 0) % ORB == iota((q, q), 1) % ORB
    small[0].wait()
    for a in range(atoms):
        for i in range(kinds):
            rows = dot_first(coup_ref[i, a], spread)
            wide = jnp.broadcast_to(rows[None, :, :tile], (tile // ORB, ORB, tile)).reshape(tile, tile)
            right[a, :, i * tile:(i + 1) * tile] = jnp.where(same_high, wide, 0.0).astype(BF)
            tall = jnp.broadcast_to(rows[:, None, tile:], (ORB, q // ORB, q)).reshape(q, q)
            left[a, i] = jnp.where(same_low, tall, 0.0).astype(BF)

    for copy in small[1:]:
        copy.wait()
    count_b, spots, ijs = phonon_ref.shape
    flat = phonon_ref[...].reshape(count_b * spots, ijs)
    row = iota((count_b * spots, width), 0)
    col = iota((count_b * spots, width), 1)
    row_fs = (row % spots) // (2 * pairs)
    row_fs = (row_fs % 2) * freqs + row_fs // 2
    fits = jnp.logical_and(row_fs == col // unit, row % per_atom == (col % block) // (2 * count_k))
    gather_rows = atoms * count_b * 2
    grow = iota((gather_rows, count_b * spots), 0)
    gcol = iota((gather_rows, count_b * spots), 1)
    gather = one_hot(jnp.logical_and(
        gcol // pairs % 2 + 2 * (gcol // spots) == grow % (2 * count_b),
        gcol % pairs // per_atom == grow // (2 * count_b),
    ))
    picked = []
    for i in range(kinds):
        pick = one_hot(iota((ijs, width), 0) == i * kinds + iota((ijs, width), 1) % unit // block)
        picked.append(dot(gather, jnp.where(fits, dot(flat, pick), 0.0).astype(BF)))
    deep = kinds * count_b * 2
    hues = 2 * count_k
    stacks = []
    for atom in range(atoms):
        rows = jnp.concatenate([p[atom * 2 * count_b:(atom + 1) * 2 * count_b] for p in picked], axis=0)
        hue = iota((deep, width), 1) % hues
        stacks.append(jnp.concatenate([jnp.where(hue == h, rows, 0.0) for h in range(hues)], axis=0).astype(BF))

    crow = iota((unit, hues * deep), 0)
    ccol = iota((unit, hues * deep), 1)
    c_row, c_col = crow % 2, ccol // deep % 2
    part, b_col = ccol % 2, ccol % (2 * count_b) // 2
    fixed = jnp.logical_and(
        crow // block == ccol % deep // (2 * count_b), part == jnp.where(c_row == c_col, 0, 1)
    )
    signed = jnp.where(fixed, jnp.where(c_row < c_col, -1.0, 1.0), 0.0)
    b_want = b_col.astype(F32)
    pick_k = one_hot(iota((unit, count_k), 1) == iota((unit, count_k), 0) % (2 * count_k) // 2)
    same_pair = iota((unit, width), 0) % block // hues == iota((unit, width), 1) % block // hues
    nk = table_ref.shape[1]

    def select(first):
        table = table_ref[...].astype(F32).astype(BF)
        k2 = iota((nk, hues * deep), 1) // (2 * deep)
        want = one_hot(iota((nk, hues * deep), 0) == first + k2)
        index = dot(dot(pick_k, table).astype(BF), want)
        return jnp.where(index == b_want, signed, 0.0).astype(BF)

    def coefficients(sel, atom):
        return jnp.where(same_pair, dot(sel, stacks[atom]), 0.0).astype(BF)

    sides = {}
    for r in range(moms):
        sel = select(lax.rem(mom + r, moms) * count_k)
        for atom in range(atoms):
            coef = coefficients(sel, atom)
            if r == 0:
                coef_own[atom] = coef
                continue
            for d in range(2):
                src, dst = iota((width, (moms - 1) * side), 0), iota((width, (moms - 1) * side), 1)
                inside = jnp.logical_and(src >= d * side, src < (d + 1) * side)
                move = one_hot(jnp.logical_and(dst - (r - 1) * side == src - d * side, inside))
                sides.setdefault((atom, d), []).append(dot(coef, move))
    for (atom, d), pieces in sides.items():
        coef_side[d, atom] = sum(pieces[1:], pieces[0]).astype(BF)

    starts = []
    for sense in range(2):
        for w in range(freqs):
            starts.append(count_e - shift_ref[w] if sense == 0 else count_e + shift_ref[w])

    tiles = q // tile

    def rotate(r, place):
        for atom in range(atoms):
            found = []
            for p in range(per_atom):
                rows = jnp.concatenate(
                    [bufs[r][:, place * count_e + e, atom * per_atom + p].reshape(2 * count_k, q) for e in range(count_e)], axis=0
                )
                rows = jnp.concatenate([rows[:, t * tile:(t + 1) * tile] for t in range(tiles)], axis=0)
                found.append(dot(rows, right[neigh_ref[p, atom]]).reshape(tiles, count_e, 2 * count_k, kinds * tile))
            for j in range(kinds):
                for t in range(tiles):
                    both = jnp.concatenate([f[t, :, :, j * tile:(j + 1) * tile] for f in found], axis=1).astype(BF)
                    rot[r, atom, pl.ds(place * count_e, count_e), j * block:(j + 1) * block, t * tile:(t + 1) * tile] = both

    def side_term(atom, d, e):
        window = jnp.concatenate(
            [rot[r, atom, e + count_e + (2 * d - 1) * shift_ref[w]] for r in range(1, moms) for w in range(freqs)], axis=0
        )
        return dot(coef_side[d, atom], window)

    own.wait()
    rotate(0, 1)
    for k in range(count_k):
        for r in range(1, moms):
            mom_copy(r, k).wait_recv()
            when_sent(r, k, start)
        late = k + split
        if late < count_k:
            @pl.when(has_far)
            def _():
                halo_copy(near, 0, late).wait_recv()
                for r in range(1, moms):
                    relay_copy(r, late).start()

    for r in range(1, moms):
        rotate(r, 1)
    for k in range(count_k):
        if k >= split:
            halo_copy(far, 0, k).wait_recv()
        else:
            @pl.when(has_prev)
            def _():
                halo_copy(0, 0, k).wait_recv()

            @pl.when(has_next)
            def _():
                halo_copy(1, 0, k).wait_recv()
    rotate(0, 0)
    rotate(0, 2)
    for atom in range(atoms):
        for e in range(count_e):
            window = jnp.concatenate([rot[0, atom, e + first] for first in starts], axis=0)
            sums[atom, e] = dot(coef_own[atom], window)
    if moms > 1:
        for r in range(1, moms):
            for k in range(count_k):
                halo_copy(far, r, k).wait_recv()
            rotate(r, 2 * far)
        for atom in range(atoms):
            for e in range(count_e):
                sums[atom, e] += side_term(atom, far, e)

        @pl.when(has_far)
        def _():
            for r in range(1, moms):
                for k in range(count_k):
                    halo_copy(near, r, k).wait_recv()

        for r in range(1, moms):
            rotate(r, 2 * near)

    for atom in range(atoms):
        for e in range(count_e):
            total = sums[atom, e]
            if moms > 1:
                total = total + side_term(atom, near, e)
            total = total.astype(BF)
            for i in range(kinds):
                half[atom, i, pl.ds(e * block, block)] = total[i * block:(i + 1) * block]
    for atom in range(atoms):
        result = None
        for i in range(kinds):
            piece = dot(half[atom, i], left[atom, i])
            result = piece if result is None else result + piece
        for e in range(count_e):
            for p in range(per_atom):
                for k in range(count_k):
                    at = e * block + (p * count_k + k) * 2
                    out_ref[k, e, atom * per_atom + p] = result[at:at + 2]

    for k in range(count_k):
        for r in range(moms):
            when_sent(r, k, lambda copy: copy.wait_send())
            if r > 0:
                mom_copy(r, k).wait_send()
                if k >= split:
                    @pl.when(has_far)
                    def _():
                        relay_copy(r, k).wait_send()


def shards(green, phonon, coupling, neighbours, momentum_table, shifts):
    moms, slabs = lax.axis_size("mom"), lax.axis_size("en")
    count_k, count_e, pairs = green.shape[:3]
    q = green.shape[4]
    kinds, atoms = coupling.shape[:2]
    ijs = phonon.shape[3]
    count_b = phonon.shape[0]
    spread = phonon.transpose(0, 1, 2, 4, 5, 3).reshape(count_b, -1, ijs)
    tile = 128
    block = pairs // atoms * count_k * 2
    unit = kinds * block
    side = shifts.shape[0] * unit
    dma = pltpu.SemaphoreType.DMA
    args = (neighbours.T, shifts, momentum_table, green, spread, coupling)
    return pl.pallas_call(
        functools.partial(kernel, moms, slabs),
        out_shape=pltpu.VMEM(green.shape, F32),
        in_specs=[pl.BlockSpec(memory_space=pltpu.HBM)] * len(args),
        out_specs=pl.BlockSpec(memory_space=pltpu.VMEM),
        scratch_shapes=[
            pltpu.SMEM(neighbours.T.shape, jnp.int32),
            pltpu.SMEM(shifts.shape, jnp.int32),
            pltpu.VMEM(momentum_table.shape, jnp.int32),
            pltpu.VMEM(spread.shape, BF),
            pltpu.VMEM(coupling.shape, BF),
            pltpu.VMEM((atoms, tile, kinds * tile), BF),
            pltpu.VMEM((atoms, kinds, q, q), BF),
            pltpu.VMEM((atoms, unit, 2 * side), BF),
            pltpu.VMEM((2, atoms, unit, max(moms - 1, 1) * side), BF),
            pltpu.VMEM((moms, atoms, 3 * count_e, unit, q), BF),
            pltpu.VMEM((atoms, count_e, unit, q), F32),
            pltpu.VMEM((atoms, kinds, count_e * block, q), BF),
            dma((5,)),
            dma,
            dma((moms, count_k)),
            dma((moms, count_k)),
            dma((2, moms, count_k)),
            dma((2, moms, count_k)),
            dma((moms, count_k)),
        ] + [pltpu.VMEM((count_k, 3 * count_e, pairs, 2, q), BF)] * moms,
        compiler_params=pltpu.CompilerParams(
            collective_id=0, has_side_effects=True, vmem_limit_bytes=48 * 1024 * 1024
        ),
    )(*[pltpu.with_memory_space_constraint(x, pltpu.HBM) for x in args])


def solution(mesh):
    return jax.shard_map(
        shards,
        mesh=mesh,
        in_specs=(P("mom", "en", None, None, None), P(), P(), P(), P("mom", None), P()),
        out_specs=P("mom", "en", None, None, None),
        check_vma=False,
    )
```

```python
import functools

import jax
import jax.numpy as jnp
from jax import lax
from jax.experimental import pallas as pl
from jax.experimental.pallas import tpu as pltpu
from jax.sharding import PartitionSpec as P

ORB = 16
MESH = pl.DeviceIdType.MESH
BF = jnp.bfloat16
F32 = jnp.float32


def dot(a, b):
    return jnp.dot(a, b, preferred_element_type=F32)


def dot_first(a, b):
    return lax.dot_general(a, b, (((0,), (0,)), ((), ())), preferred_element_type=F32)


def iota(shape, dim):
    return lax.broadcasted_iota(jnp.int32, shape, dim)


def one_hot(mask):
    return jnp.where(mask, 1.0, 0.0).astype(BF)


def kernel(moms, slabs, neigh_any, shift_any, table_any, green_ref, phonon_any, coup_any, out_ref,
           neigh_ref, shift_ref, table_ref, phonon_ref, coup_ref, right, left, coef_own, coef_side,
           rot, sums, half, small_sem, own_sem, send_mom, recv_mom, send_halo, recv_halo, send_relay, *bufs):
    mom = lax.axis_index("mom")
    en = lax.axis_index("en")
    count_k, count_e, pairs = green_ref.shape[0], green_ref.shape[1], green_ref.shape[2]
    q = green_ref.shape[4]
    kinds, atoms = coup_ref.shape[0], coup_ref.shape[1]
    per_atom = pairs // atoms
    freqs = shift_ref.shape[0]
    block = per_atom * count_k * 2
    unit = kinds * block
    side = freqs * unit
    width = 2 * side
    tile = right.shape[1]
    has_prev = en > 0
    has_next = en < slabs - 1

    own = pltpu.make_async_copy(green_ref, bufs[0].at[:, pl.ds(count_e, count_e)], own_sem)

    barrier = pltpu.get_barrier_semaphore()

    def mom_peer(r):
        return {"mom": lax.rem(mom + moms - r, moms)}

    for r in range(1, moms):
        pl.semaphore_signal(barrier, inc=1, device_id=mom_peer(r), device_id_type=MESH)

    @pl.when(has_prev)
    def _():
        pl.semaphore_signal(barrier, inc=1, device_id={"en": en - 1}, device_id_type=MESH)

    @pl.when(has_next)
    def _():
        pl.semaphore_signal(barrier, inc=1, device_id={"en": en + 1}, device_id_type=MESH)

    pl.semaphore_wait(
        barrier, moms - 1 + jnp.where(has_prev, 1, 0) + jnp.where(has_next, 1, 0)
    )

    def mom_copy(r, k):
        return pltpu.make_async_remote_copy(
            src_ref=green_ref.at[k],
            dst_ref=bufs[r].at[k, pl.ds(count_e, count_e)],
            send_sem=send_mom.at[r, k],
            recv_sem=recv_mom.at[r, k],
            device_id=mom_peer(r),
            device_id_type=MESH,
        )

    def halo_copy(d, r, k):
        src = green_ref.at[k] if r == 0 else bufs[r].at[k, pl.ds(count_e, count_e)]
        return pltpu.make_async_remote_copy(
            src_ref=src,
            dst_ref=bufs[r].at[k, pl.ds(2 * count_e * d, count_e)],
            send_sem=send_halo.at[d, r, k],
            recv_sem=recv_halo.at[d, r, k],
            device_id={"en": en + 1 - 2 * d},
            device_id_type=MESH,
        )

    small = [
        pltpu.make_async_copy(src, dst, small_sem.at[i])
        for i, (src, dst) in enumerate([
            (coup_any, coup_ref), (phonon_any, phonon_ref), (table_any, table_ref),
            (neigh_any, neigh_ref), (shift_any, shift_ref),
        ])
    ]

    near = en % 2
    far = 1 - near
    has_far = jnp.where(near == 0, has_prev, has_next)
    split = count_k // 2

    def relay_copy(r, k):
        place = pl.ds(2 * count_e * near, count_e)
        return pltpu.make_async_remote_copy(
            src_ref=bufs[0].at[k, place],
            dst_ref=bufs[r].at[k, place],
            send_sem=send_relay.at[r, k],
            recv_sem=recv_halo.at[near, r, k],
            device_id=mom_peer(r),
            device_id_type=MESH,
        )

    def when_sent(r, k, act):
        if r == 0 or k < split:
            @pl.when(has_next)
            def _():
                act(halo_copy(0, r, k))

            @pl.when(has_prev)
            def _():
                act(halo_copy(1, r, k))
        else:
            act(halo_copy(near, r, k))

    start = lambda copy: copy.start()
    for k in range(count_k):
        for r in range(1, moms):
            mom_copy(r, k).start()
        when_sent(0, (k + split) % count_k, start)
    for copy in small:
        copy.start()
    own.start()

    @pl.when(jnp.logical_not(has_prev))
    def _():
        for r in range(moms):
            for k in range(count_k):
                bufs[r][k, pl.ds(0, count_e)] = jnp.zeros((count_e, pairs, 2, q), BF)

    @pl.when(jnp.logical_not(has_next))
    def _():
        for r in range(moms):
            for k in range(count_k):
                bufs[r][k, pl.ds(2 * count_e, count_e)] = jnp.zeros((count_e, pairs, 2, q), BF)

    lane = iota((ORB, tile + q), 1)
    spread = one_hot(jnp.where(lane < tile, lane % ORB, (lane - tile) // ORB) == iota((ORB, tile + q), 0))
    same_high = iota((tile, tile), 0) // ORB == iota((tile, tile), 1) // ORB
    same_low = iota((q, q), 0) % ORB == iota((q, q), 1) % ORB
    small[0].wait()
    for a in range(atoms):
        for i in range(kinds):
            rows = dot_first(coup_ref[i, a], spread)
            wide = jnp.broadcast_to(rows[None, :, :tile], (tile // ORB, ORB, tile)).reshape(tile, tile)
            right[a, :, i * tile:(i + 1) * tile] = jnp.where(same_high, wide, 0.0).astype(BF)
            tall = jnp.broadcast_to(rows[:, None, tile:], (ORB, q // ORB, q)).reshape(q, q)
            left[a, i] = jnp.where(same_low, tall, 0.0).astype(BF)

    for copy in small[1:]:
        copy.wait()
    count_b, spots, ijs = phonon_ref.shape
    flat = phonon_ref[...].reshape(count_b * spots, ijs)
    row = iota((count_b * spots, width), 0)
    col = iota((count_b * spots, width), 1)
    row_fs = (row % spots) // (2 * pairs)
    row_fs = (row_fs % 2) * freqs + row_fs // 2
    fits = jnp.logical_and(row_fs == col // unit, row % per_atom == (col % block) // (2 * count_k))
    gather_rows = atoms * count_b * 2
    grow = iota((gather_rows, count_b * spots), 0)
    gcol = iota((gather_rows, count_b * spots), 1)
    gather = one_hot(jnp.logical_and(
        gcol // pairs % 2 + 2 * (gcol // spots) == grow % (2 * count_b),
        gcol % pairs // per_atom == grow // (2 * count_b),
    ))
    picked = []
    for i in range(kinds):
        pick = one_hot(iota((ijs, width), 0) == i * kinds + iota((ijs, width), 1) % unit // block)
        picked.append(dot(gather, jnp.where(fits, dot(flat, pick), 0.0).astype(BF)))
    deep = kinds * count_b * 2
    hues = 2 * count_k
    stacks = []
    for atom in range(atoms):
        rows = jnp.concatenate([p[atom * 2 * count_b:(atom + 1) * 2 * count_b] for p in picked], axis=0)
        hue = iota((deep, width), 1) % hues
        stacks.append(jnp.concatenate([jnp.where(hue == h, rows, 0.0) for h in range(hues)], axis=0).astype(BF))

    crow = iota((unit, hues * deep), 0)
    ccol = iota((unit, hues * deep), 1)
    c_row, c_col = crow % 2, ccol // deep % 2
    part, b_col = ccol % 2, ccol % (2 * count_b) // 2
    fixed = jnp.logical_and(
        crow // block == ccol % deep // (2 * count_b), part == jnp.where(c_row == c_col, 0, 1)
    )
    signed = jnp.where(fixed, jnp.where(c_row < c_col, -1.0, 1.0), 0.0)
    b_want = b_col.astype(F32)
    pick_k = one_hot(iota((unit, count_k), 1) == iota((unit, count_k), 0) % (2 * count_k) // 2)
    same_pair = iota((unit, width), 0) % block // hues == iota((unit, width), 1) % block // hues
    nk = table_ref.shape[1]

    def select(first):
        table = table_ref[...].astype(F32).astype(BF)
        k2 = iota((nk, hues * deep), 1) // (2 * deep)
        want = one_hot(iota((nk, hues * deep), 0) == first + k2)
        index = dot(dot(pick_k, table).astype(BF), want)
        return jnp.where(index == b_want, signed, 0.0).astype(BF)

    def coefficients(sel, atom):
        return jnp.where(same_pair, dot(sel, stacks[atom]), 0.0).astype(BF)

    sides = {}
    for r in range(moms):
        sel = select(lax.rem(mom + r, moms) * count_k)
        count = moms - 1 if r > 0 else 1
        at = max(r - 1, 0) * side
        for atom in range(atoms):
            coef = coefficients(sel, atom)
            for d in range(2):
                src, dst = iota((width, count * side), 0), iota((width, count * side), 1)
                inside = jnp.logical_and(src >= d * side, src < (d + 1) * side)
                move = one_hot(jnp.logical_and(dst - at == src - d * side, inside))
                sides.setdefault((min(r, 1), d, atom), []).append(dot(coef, move))
    for (others, d, atom), pieces in sides.items():
        (coef_side if others else coef_own)[d, atom] = sum(pieces[1:], pieces[0]).astype(BF)

    tiles = q // tile

    def rotate(r, place):
        for atom in range(atoms):
            found = []
            for p in range(per_atom):
                rows = jnp.concatenate(
                    [bufs[r][:, place * count_e + e, atom * per_atom + p].reshape(2 * count_k, q) for e in range(count_e)], axis=0
                )
                rows = jnp.concatenate([rows[:, t * tile:(t + 1) * tile] for t in range(tiles)], axis=0)
                found.append(dot(rows, right[neigh_ref[p, atom]]).reshape(tiles, count_e, 2 * count_k, kinds * tile))
            for j in range(kinds):
                for t in range(tiles):
                    both = jnp.concatenate([f[t, :, :, j * tile:(j + 1) * tile] for f in found], axis=1).astype(BF)
                    rot[r, atom, pl.ds(place * count_e, count_e), j * block:(j + 1) * block, t * tile:(t + 1) * tile] = both

    def term(coef, group, atom, d, e):
        window = jnp.concatenate(
            [rot[r, atom, e + count_e + (2 * d - 1) * shift_ref[w]] for r in group for w in range(freqs)], axis=0
        )
        return dot(coef[d, atom], window)

    rest = range(1, moms)

    def add(coef, group, d, fresh=False):
        for atom in range(atoms):
            for e in range(count_e):
                piece = term(coef, group, atom, d, e)
                sums[atom, e] = piece if fresh else sums[atom, e] + piece

    own.wait()
    rotate(0, 1)
    for k in range(count_k):
        halo_copy(far, 0, k).wait_recv()
    rotate(0, 2 * far)
    add(coef_own, [0], far, True)
    for k in range(count_k):
        for r in rest:
            mom_copy(r, k).wait_recv()
            when_sent(r, k, start)
        late = k + split
        if late < count_k:
            @pl.when(has_far)
            def _():
                halo_copy(near, 0, late).wait_recv()
                for r in rest:
                    relay_copy(r, late).start()

    for r in rest:
        rotate(r, 1)

    @pl.when(has_far)
    def _():
        for k in range(split):
            halo_copy(near, 0, k).wait_recv()

    rotate(0, 2 * near)
    add(coef_own, [0], near)
    if moms > 1:
        for r in rest:
            for k in range(count_k):
                halo_copy(far, r, k).wait_recv()
            rotate(r, 2 * far)
        add(coef_side, rest, far)

        @pl.when(has_far)
        def _():
            for r in rest:
                for k in range(count_k):
                    halo_copy(near, r, k).wait_recv()

        for r in rest:
            rotate(r, 2 * near)

    for atom in range(atoms):
        for e in range(count_e):
            total = sums[atom, e]
            if moms > 1:
                total = total + term(coef_side, rest, atom, near, e)
            total = total.astype(BF)
            for i in range(kinds):
                half[atom, i, pl.ds(e * block, block)] = total[i * block:(i + 1) * block]
    for atom in range(atoms):
        result = None
        for i in range(kinds):
            piece = dot(half[atom, i], left[atom, i])
            result = piece if result is None else result + piece
        for e in range(count_e):
            for p in range(per_atom):
                for k in range(count_k):
                    at = e * block + (p * count_k + k) * 2
                    out_ref[k, e, atom * per_atom + p] = result[at:at + 2]

    for k in range(count_k):
        for r in range(moms):
            when_sent(r, k, lambda copy: copy.wait_send())
            if r > 0:
                mom_copy(r, k).wait_send()
                if k >= split:
                    @pl.when(has_far)
                    def _():
                        relay_copy(r, k).wait_send()


def shards(green, phonon, coupling, neighbours, momentum_table, shifts):
    moms, slabs = lax.axis_size("mom"), lax.axis_size("en")
    count_k, count_e, pairs = green.shape[:3]
    q = green.shape[4]
    kinds, atoms = coupling.shape[:2]
    ijs = phonon.shape[3]
    count_b = phonon.shape[0]
    spread = phonon.transpose(0, 1, 2, 4, 5, 3).reshape(count_b, -1, ijs)
    tile = 128
    block = pairs // atoms * count_k * 2
    unit = kinds * block
    side = shifts.shape[0] * unit
    dma = pltpu.SemaphoreType.DMA
    args = (neighbours.T, shifts, momentum_table, green, spread, coupling)
    return pl.pallas_call(
        functools.partial(kernel, moms, slabs),
        out_shape=pltpu.VMEM(green.shape, F32),
        in_specs=[pl.BlockSpec(memory_space=pltpu.HBM)] * len(args),
        out_specs=pl.BlockSpec(memory_space=pltpu.VMEM),
        scratch_shapes=[
            pltpu.SMEM(neighbours.T.shape, jnp.int32),
            pltpu.SMEM(shifts.shape, jnp.int32),
            pltpu.VMEM(momentum_table.shape, jnp.int32),
            pltpu.VMEM(spread.shape, BF),
            pltpu.VMEM(coupling.shape, BF),
            pltpu.VMEM((atoms, tile, kinds * tile), BF),
            pltpu.VMEM((atoms, kinds, q, q), BF),
            pltpu.VMEM((2, atoms, unit, side), BF),
            pltpu.VMEM((2, atoms, unit, max(moms - 1, 1) * side), BF),
            pltpu.VMEM((moms, atoms, 3 * count_e, unit, q), BF),
            pltpu.VMEM((atoms, count_e, unit, q), F32),
            pltpu.VMEM((atoms, kinds, count_e * block, q), BF),
            dma((5,)),
            dma,
            dma((moms, count_k)),
            dma((moms, count_k)),
            dma((2, moms, count_k)),
            dma((2, moms, count_k)),
            dma((moms, count_k)),
        ] + [pltpu.VMEM((count_k, 3 * count_e, pairs, 2, q), BF)] * moms,
        compiler_params=pltpu.CompilerParams(
            collective_id=0, has_side_effects=True, vmem_limit_bytes=48 * 1024 * 1024
        ),
    )(*[pltpu.with_memory_space_constraint(x, pltpu.HBM) for x in args])


def solution(mesh):
    return jax.shard_map(
        shards,
        mesh=mesh,
        in_specs=(P("mom", "en", None, None, None), P(), P(), P(), P("mom", None), P()),
        out_specs=P("mom", "en", None, None, None),
        check_vma=False,
    )
```

```python
import functools

import jax
import jax.numpy as jnp
from jax import lax
from jax.experimental import pallas as pl
from jax.experimental.pallas import tpu as pltpu
from jax.sharding import PartitionSpec as P

ORB = 16
MESH = pl.DeviceIdType.MESH
BF = jnp.bfloat16
F32 = jnp.float32


def dot(a, b):
    return jnp.dot(a, b, preferred_element_type=F32)


def dot_first(a, b):
    return lax.dot_general(a, b, (((0,), (0,)), ((), ())), preferred_element_type=F32)


def iota(shape, dim):
    return lax.broadcasted_iota(jnp.int32, shape, dim)


def one_hot(mask):
    return jnp.where(mask, 1.0, 0.0).astype(BF)


def kernel(moms, slabs, neigh_any, shift_any, table_any, green_ref, phonon_any, coup_any, out_ref,
           neigh_ref, shift_ref, table_ref, phonon_ref, coup_ref, right, left, coef_own, coef_side,
           sums, small_sem, own_sem, send_mom, recv_mom, send_halo, recv_halo, send_relay, *many):
    mom = lax.axis_index("mom")
    en = lax.axis_index("en")
    count_k, count_e, pairs = green_ref.shape[0], green_ref.shape[1], green_ref.shape[2]
    q = green_ref.shape[4]
    kinds, atoms = coup_ref.shape[0], coup_ref.shape[1]
    per_atom = pairs // atoms
    freqs = shift_ref.shape[0]
    block = per_atom * count_k * 2
    unit = kinds * block
    side = freqs * unit
    width = 2 * side
    tile = right.shape[1]
    bufs, rots = many[:moms], many[moms:]
    has_prev = en > 0
    has_next = en < slabs - 1

    own = pltpu.make_async_copy(green_ref, bufs[0].at[:, pl.ds(count_e, count_e)], own_sem)

    barrier = pltpu.get_barrier_semaphore()

    def mom_peer(r):
        return {"mom": lax.rem(mom + moms - r, moms)}

    for r in range(1, moms):
        pl.semaphore_signal(barrier, inc=1, device_id=mom_peer(r), device_id_type=MESH)

    @pl.when(has_prev)
    def _():
        pl.semaphore_signal(barrier, inc=1, device_id={"en": en - 1}, device_id_type=MESH)

    @pl.when(has_next)
    def _():
        pl.semaphore_signal(barrier, inc=1, device_id={"en": en + 1}, device_id_type=MESH)

    small = [
        pltpu.make_async_copy(src, dst, small_sem.at[i])
        for i, (src, dst) in enumerate([
            (coup_any, coup_ref), (phonon_any, phonon_ref), (table_any, table_ref),
            (neigh_any, neigh_ref), (shift_any, shift_ref),
        ])
    ]

    for copy in small:
        copy.start()
    own.start()

    pl.semaphore_wait(
        barrier, moms - 1 + jnp.where(has_prev, 1, 0) + jnp.where(has_next, 1, 0)
    )

    def mom_copy(r, k):
        return pltpu.make_async_remote_copy(
            src_ref=green_ref.at[k],
            dst_ref=bufs[r].at[k, pl.ds(count_e, count_e)],
            send_sem=send_mom.at[r, k],
            recv_sem=recv_mom.at[r, k],
            device_id=mom_peer(r),
            device_id_type=MESH,
        )

    def halo_copy(d, r, k):
        src = green_ref.at[k] if r == 0 else bufs[r].at[k, pl.ds(count_e, count_e)]
        return pltpu.make_async_remote_copy(
            src_ref=src,
            dst_ref=bufs[r].at[k, pl.ds(2 * count_e * d, count_e)],
            send_sem=send_halo.at[d, r, k],
            recv_sem=recv_halo.at[d, r, k],
            device_id={"en": en + 1 - 2 * d},
            device_id_type=MESH,
        )

    near = en % 2
    far = 1 - near
    has_far = jnp.where(near == 0, has_prev, has_next)
    split = count_k // 2

    def relay_copy(r, k):
        place = pl.ds(2 * count_e * near, count_e)
        return pltpu.make_async_remote_copy(
            src_ref=bufs[0].at[k, place],
            dst_ref=bufs[r].at[k, place],
            send_sem=send_relay.at[r, k],
            recv_sem=recv_halo.at[near, r, k],
            device_id=mom_peer(r),
            device_id_type=MESH,
        )

    def when_sent(r, k, act):
        if r == 0 or k < split:
            @pl.when(has_next)
            def _():
                act(halo_copy(0, r, k))

            @pl.when(has_prev)
            def _():
                act(halo_copy(1, r, k))
        else:
            act(halo_copy(near, r, k))

    for k in range(count_k):
        for r in range(1, moms):
            mom_copy(r, k).start()

        @pl.when(has_far)
        def _():
            halo_copy(far, 0, (k + split) % count_k).start()

    for k in range(count_k):
        halo_copy(near, 0, k).start()

    @pl.when(jnp.logical_not(has_prev))
    def _():
        for r in range(moms):
            for k in range(count_k):
                bufs[r][k, pl.ds(0, count_e)] = jnp.zeros((count_e, pairs, 2, q), BF)

    @pl.when(jnp.logical_not(has_next))
    def _():
        for r in range(moms):
            for k in range(count_k):
                bufs[r][k, pl.ds(2 * count_e, count_e)] = jnp.zeros((count_e, pairs, 2, q), BF)

    lane = iota((ORB, tile + q), 1)
    spread = one_hot(jnp.where(lane < tile, lane % ORB, (lane - tile) // ORB) == iota((ORB, tile + q), 0))
    same_high = iota((tile, tile), 0) // ORB == iota((tile, tile), 1) // ORB
    same_low = iota((q, q), 0) % ORB == iota((q, q), 1) % ORB
    small[0].wait()
    for a in range(atoms):
        for i in range(kinds):
            rows = dot_first(coup_ref[i, a], spread)
            wide = jnp.broadcast_to(rows[None, :, :tile], (tile // ORB, ORB, tile)).reshape(tile, tile)
            right[a, :, i * tile:(i + 1) * tile] = jnp.where(same_high, wide, 0.0).astype(BF)
            tall = jnp.broadcast_to(rows[:, None, tile:], (ORB, q // ORB, q)).reshape(q, q)
            left[a, i * q:(i + 1) * q] = jnp.where(same_low, tall, 0.0).astype(BF)

    for copy in small[1:]:
        copy.wait()
    count_b, spots, ijs = phonon_ref.shape
    flat = phonon_ref[...].reshape(count_b * spots, ijs)
    row = iota((count_b * spots, width), 0)
    col = iota((count_b * spots, width), 1)
    row_fs = (row % spots) // (2 * pairs)
    row_fs = (row_fs % 2) * freqs + row_fs // 2
    fits = jnp.logical_and(row_fs == col // unit, row % per_atom == (col % block) // (2 * count_k))
    gather_rows = atoms * count_b * 2
    grow = iota((gather_rows, count_b * spots), 0)
    gcol = iota((gather_rows, count_b * spots), 1)
    gather = one_hot(jnp.logical_and(
        gcol // pairs % 2 + 2 * (gcol // spots) == grow % (2 * count_b),
        gcol % pairs // per_atom == grow // (2 * count_b),
    ))
    picked = []
    for i in range(kinds):
        pick = one_hot(iota((ijs, width), 0) == i * kinds + iota((ijs, width), 1) % unit // block)
        picked.append(dot(gather, jnp.where(fits, dot(flat, pick), 0.0).astype(BF)))
    deep = kinds * count_b * 2
    hues = 2 * count_k
    stacks = []
    for atom in range(atoms):
        rows = jnp.concatenate([p[atom * 2 * count_b:(atom + 1) * 2 * count_b] for p in picked], axis=0)
        hue = iota((deep, width), 1) % hues
        stacks.append(jnp.concatenate([jnp.where(hue == h, rows, 0.0) for h in range(hues)], axis=0).astype(BF))

    crow = iota((unit, hues * deep), 0)
    ccol = iota((unit, hues * deep), 1)
    c_row, c_col = crow % 2, ccol // deep % 2
    part, b_col = ccol % 2, ccol % (2 * count_b) // 2
    fixed = jnp.logical_and(
        crow // block == ccol % deep // (2 * count_b), part == jnp.where(c_row == c_col, 0, 1)
    )
    signed = jnp.where(fixed, jnp.where(c_row < c_col, -1.0, 1.0), 0.0)
    b_want = b_col.astype(F32)
    pick_k = one_hot(iota((unit, count_k), 1) == iota((unit, count_k), 0) % (2 * count_k) // 2)
    same_pair = iota((unit, width), 0) % block // hues == iota((unit, width), 1) % block // hues
    nk = table_ref.shape[1]

    def select(first):
        table = table_ref[...].astype(F32).astype(BF)
        k2 = iota((nk, hues * deep), 1) // (2 * deep)
        want = one_hot(iota((nk, hues * deep), 0) == first + k2)
        index = dot(dot(pick_k, table).astype(BF), want)
        return jnp.where(index == b_want, signed, 0.0).astype(BF)

    def coefficients(sel, atom):
        return jnp.where(same_pair, dot(sel, stacks[atom]), 0.0).astype(BF)

    sides = {}
    for r in range(moms):
        sel = select(lax.rem(mom + r, moms) * count_k)
        count = moms - 1 if r > 0 else 1
        at = max(r - 1, 0) * side
        for atom in range(atoms):
            coef = coefficients(sel, atom)
            for d in range(2):
                src, dst = iota((width, count * side), 0), iota((width, count * side), 1)
                inside = jnp.logical_and(src >= d * side, src < (d + 1) * side)
                move = one_hot(jnp.logical_and(dst - at == src - d * side, inside))
                sides.setdefault((min(r, 1), d, atom), []).append(dot(coef, move))
    for (others, d, atom), pieces in sides.items():
        (coef_side if others else coef_own)[d, atom] = sum(pieces[1:], pieces[0]).astype(BF)

    tiles = q // tile

    def rotate(r, place, members=range(atoms)):
        for atom in members:
            found = []
            for p in range(per_atom):
                rows = jnp.concatenate(
                    [bufs[r][:, place * count_e + e, atom * per_atom + p].reshape(2 * count_k, q) for e in range(count_e)], axis=0
                )
                rows = jnp.concatenate([rows[:, t * tile:(t + 1) * tile] for t in range(tiles)], axis=0)
                found.append(dot(rows, right[neigh_ref[p, atom]]).reshape(tiles, count_e, 2 * count_k, kinds * tile))
            for j in range(kinds):
                for t in range(tiles):
                    both = jnp.concatenate([f[t, :, :, j * tile:(j + 1) * tile] for f in found], axis=1).astype(BF)
                    rots[atom][r, pl.ds(place * count_e, count_e), j * block:(j + 1) * block, t * tile:(t + 1) * tile] = both

    def term(coef, group, atom, d, e):
        window = jnp.concatenate(
            [rots[atom][r, e + count_e + (2 * d - 1) * shift_ref[w]] for r in group for w in range(freqs)], axis=0
        )
        return dot(coef[d, atom], window)

    rest = range(1, moms)

    def add(coef, group, d, fresh=False):
        for atom in range(atoms):
            for e in range(count_e):
                piece = term(coef, group, atom, d, e)
                sums[atom, e] = piece if fresh else sums[atom, e] + piece

    own.wait()
    rotate(0, 1)
    for k in range(count_k):
        halo_copy(far, 0, k).wait_recv()
    rotate(0, 2 * far)
    add(coef_own, [0], far, True)
    for k in range(count_k):
        for r in rest:
            mom_copy(r, k).wait_recv()
            if k < split:
                @pl.when(has_far)
                def _():
                    halo_copy(far, r, k).start()
        late = k + split
        if late < count_k:
            @pl.when(has_far)
            def _():
                halo_copy(near, 0, late).wait_recv()
                for r in rest:
                    relay_copy(r, late).start()
        for r in rest:
            halo_copy(near, r, k).start()

    for r in rest:
        rotate(r, 1)

    @pl.when(has_far)
    def _():
        for k in range(split):
            halo_copy(near, 0, k).wait_recv()

    rotate(0, 2 * near)
    add(coef_own, [0], near)
    if moms > 1:
        for r in rest:
            for k in range(count_k):
                halo_copy(far, r, k).wait_recv()
            rotate(r, 2 * far)
        add(coef_side, rest, far)

        @pl.when(has_far)
        def _():
            for r in rest:
                for k in range(count_k):
                    halo_copy(near, r, k).wait_recv()

    def turn(atom):
        for r in rest:
            rotate(r, 2 * near, [atom])

    halves = {}

    def close(atom):
        rows = [[] for _ in range(kinds)]
        for e in range(count_e):
            total = sums[atom, e]
            if moms > 1:
                total = total + term(coef_side, rest, atom, near, e)
            total = total.astype(BF)
            for i in range(kinds):
                rows[i].append(total[i * block:(i + 1) * block])
        halves[atom] = [jnp.concatenate(row, axis=0) for row in rows]

    def finish(atom):
        result = dot(jnp.concatenate(halves.pop(atom), axis=1), left[atom])
        for e in range(count_e):
            for p in range(per_atom):
                for k in range(count_k):
                    at = e * block + (p * count_k + k) * 2
                    out_ref[k, e, atom * per_atom + p] = result[at:at + 2]

    steps = [turn, close, finish]
    for step in steps:
        for atom in range(atoms):
            step(atom)

    for k in range(count_k):
        for r in range(moms):
            when_sent(r, k, lambda copy: copy.wait_send())
            if r > 0:
                mom_copy(r, k).wait_send()
                if k >= split:
                    @pl.when(has_far)
                    def _():
                        relay_copy(r, k).wait_send()


def shards(green, phonon, coupling, neighbours, momentum_table, shifts):
    moms, slabs = lax.axis_size("mom"), lax.axis_size("en")
    count_k, count_e, pairs = green.shape[:3]
    q = green.shape[4]
    kinds, atoms = coupling.shape[:2]
    ijs = phonon.shape[3]
    count_b = phonon.shape[0]
    spread = phonon.transpose(0, 1, 2, 4, 5, 3).reshape(count_b, -1, ijs)
    tile = 128
    block = pairs // atoms * count_k * 2
    unit = kinds * block
    side = shifts.shape[0] * unit
    dma = pltpu.SemaphoreType.DMA
    args = (neighbours.T, shifts, momentum_table, green, spread, coupling)
    return pl.pallas_call(
        functools.partial(kernel, moms, slabs),
        out_shape=pltpu.VMEM(green.shape, F32),
        in_specs=[pl.BlockSpec(memory_space=pltpu.HBM)] * len(args),
        out_specs=pl.BlockSpec(memory_space=pltpu.VMEM),
        scratch_shapes=[
            pltpu.SMEM(neighbours.T.shape, jnp.int32),
            pltpu.SMEM(shifts.shape, jnp.int32),
            pltpu.VMEM(momentum_table.shape, jnp.int32),
            pltpu.VMEM(spread.shape, BF),
            pltpu.VMEM(coupling.shape, BF),
            pltpu.VMEM((atoms, tile, kinds * tile), BF),
            pltpu.VMEM((atoms, kinds * q, q), BF),
            pltpu.VMEM((2, atoms, unit, side), BF),
            pltpu.VMEM((2, atoms, unit, max(moms - 1, 1) * side), BF),
            pltpu.VMEM((atoms, count_e, unit, q), F32),
            dma((5,)),
            dma,
            dma((moms, count_k)),
            dma((moms, count_k)),
            dma((2, moms, count_k)),
            dma((2, moms, count_k)),
            dma((moms, count_k)),
        ] + [pltpu.VMEM((count_k, 3 * count_e, pairs, 2, q), BF)] * moms
        + [pltpu.VMEM((moms, 3 * count_e, unit, q), BF)] * atoms,
        compiler_params=pltpu.CompilerParams(
            collective_id=0, has_side_effects=True, vmem_limit_bytes=48 * 1024 * 1024
        ),
    )(*[pltpu.with_memory_space_constraint(x, pltpu.HBM) for x in args])


def solution(mesh):
    return jax.shard_map(
        shards,
        mesh=mesh,
        in_specs=(P("mom", "en", None, None, None), P(), P(), P(), P("mom", None), P()),
        out_specs=P("mom", "en", None, None, None),
        check_vma=False,
    )
```

```python
import functools

import jax
import jax.numpy as jnp
from jax import lax
from jax.experimental import pallas as pl
from jax.experimental.pallas import tpu as pltpu
from jax.sharding import PartitionSpec as P

ORB = 16
MESH = pl.DeviceIdType.MESH
BF = jnp.bfloat16
F32 = jnp.float32


def dot(a, b):
    return jnp.dot(a, b, preferred_element_type=F32)


def dot_first(a, b):
    return lax.dot_general(a, b, (((0,), (0,)), ((), ())), preferred_element_type=F32)


def iota(shape, dim):
    return lax.broadcasted_iota(jnp.int32, shape, dim)


def one_hot(mask):
    return jnp.where(mask, 1.0, 0.0).astype(BF)


def kernel(moms, slabs, neigh_any, shift_any, table_any, green_ref, phonon_any, coup_any, out_ref,
           neigh_ref, shift_ref, table_ref, phonon_ref, coup_ref, right, left, coef_own, coef_side,
           sums, small_sem, own_sem, send_mom, recv_mom, send_halo, recv_halo, send_relay, *many):
    mom = lax.axis_index("mom")
    en = lax.axis_index("en")
    count_k, count_e, pairs = green_ref.shape[0], green_ref.shape[1], green_ref.shape[2]
    q = green_ref.shape[4]
    kinds, atoms = coup_ref.shape[0], coup_ref.shape[1]
    per_atom = pairs // atoms
    freqs = shift_ref.shape[0]
    block = per_atom * count_k * 2
    unit = kinds * block
    side = freqs * unit
    width = 2 * side
    tile = right.shape[1]
    bufs, rots = many[:moms], many[moms:]
    has_prev = en > 0
    has_next = en < slabs - 1

    own = pltpu.make_async_copy(green_ref, bufs[0].at[:, pl.ds(count_e, count_e)], own_sem)

    run = 1 if count_k % 2 else count_k // 2
    turns = count_k // run

    def several(k):
        return pl.ds(k * run, run)

    barrier = pltpu.get_barrier_semaphore()

    def mom_peer(r):
        return {"mom": lax.rem(mom + moms - r, moms)}

    for r in range(1, moms):
        pl.semaphore_signal(barrier, inc=1, device_id=mom_peer(r), device_id_type=MESH)

    @pl.when(has_prev)
    def _():
        pl.semaphore_signal(barrier, inc=1, device_id={"en": en - 1}, device_id_type=MESH)

    @pl.when(has_next)
    def _():
        pl.semaphore_signal(barrier, inc=1, device_id={"en": en + 1}, device_id_type=MESH)

    small = [
        pltpu.make_async_copy(src, dst, small_sem.at[i])
        for i, (src, dst) in enumerate([
            (coup_any, coup_ref), (phonon_any, phonon_ref), (table_any, table_ref),
            (neigh_any, neigh_ref), (shift_any, shift_ref),
        ])
    ]

    for copy in small:
        copy.start()
    own.start()

    pl.semaphore_wait(
        barrier, moms - 1 + jnp.where(has_prev, 1, 0) + jnp.where(has_next, 1, 0)
    )

    def mom_copy(r, k):
        return pltpu.make_async_remote_copy(
            src_ref=green_ref.at[several(k)],
            dst_ref=bufs[r].at[several(k), pl.ds(count_e, count_e)],
            send_sem=send_mom.at[r, k],
            recv_sem=recv_mom.at[r, k],
            device_id=mom_peer(r),
            device_id_type=MESH,
        )

    def halo_copy(d, r, k):
        src = green_ref.at[several(k)] if r == 0 else bufs[r].at[several(k), pl.ds(count_e, count_e)]
        return pltpu.make_async_remote_copy(
            src_ref=src,
            dst_ref=bufs[r].at[several(k), pl.ds(2 * count_e * d, count_e)],
            send_sem=send_halo.at[d, r, k],
            recv_sem=recv_halo.at[d, r, k],
            device_id={"en": en + 1 - 2 * d},
            device_id_type=MESH,
        )

    near = en % 2
    far = 1 - near
    has_far = jnp.where(near == 0, has_prev, has_next)
    split = turns // 2

    def relay_copy(r, k):
        place = pl.ds(2 * count_e * near, count_e)
        return pltpu.make_async_remote_copy(
            src_ref=bufs[0].at[several(k), place],
            dst_ref=bufs[r].at[several(k), place],
            send_sem=send_relay.at[r, k],
            recv_sem=recv_halo.at[near, r, k],
            device_id=mom_peer(r),
            device_id_type=MESH,
        )

    def when_sent(r, k, act):
        if r == 0 or k < split:
            @pl.when(has_next)
            def _():
                act(halo_copy(0, r, k))

            @pl.when(has_prev)
            def _():
                act(halo_copy(1, r, k))
        else:
            act(halo_copy(near, r, k))

    for k in range(turns):
        for r in range(1, moms):
            mom_copy(r, k).start()

        @pl.when(has_far)
        def _():
            halo_copy(far, 0, (k + split) % turns).start()

    for k in range(turns):
        halo_copy(near, 0, k).start()

    @pl.when(jnp.logical_not(has_prev))
    def _():
        for r in range(moms):
            for k in range(count_k):
                bufs[r][k, pl.ds(0, count_e)] = jnp.zeros((count_e, pairs, 2, q), BF)

    @pl.when(jnp.logical_not(has_next))
    def _():
        for r in range(moms):
            for k in range(count_k):
                bufs[r][k, pl.ds(2 * count_e, count_e)] = jnp.zeros((count_e, pairs, 2, q), BF)

    lane = iota((ORB, tile + q), 1)
    spread = one_hot(jnp.where(lane < tile, lane % ORB, (lane - tile) // ORB) == iota((ORB, tile + q), 0))
    same_high = iota((tile, tile), 0) // ORB == iota((tile, tile), 1) // ORB
    same_low = iota((q, q), 0) % ORB == iota((q, q), 1) % ORB
    small[0].wait()
    for a in range(atoms):
        for i in range(kinds):
            rows = dot_first(coup_ref[i, a], spread)
            wide = jnp.broadcast_to(rows[None, :, :tile], (tile // ORB, ORB, tile)).reshape(tile, tile)
            right[a, :, i * tile:(i + 1) * tile] = jnp.where(same_high, wide, 0.0).astype(BF)
            tall = jnp.broadcast_to(rows[:, None, tile:], (ORB, q // ORB, q)).reshape(q, q)
            left[a, i * q:(i + 1) * q] = jnp.where(same_low, tall, 0.0).astype(BF)

    for copy in small[1:]:
        copy.wait()
    count_b, spots, ijs = phonon_ref.shape
    flat = phonon_ref[...].reshape(count_b * spots, ijs)
    row = iota((count_b * spots, width), 0)
    col = iota((count_b * spots, width), 1)
    row_fs = (row % spots) // (2 * pairs)
    row_fs = (row_fs % 2) * freqs + row_fs // 2
    fits = jnp.logical_and(row_fs == col // unit, row % per_atom == (col % block) // (2 * count_k))
    gather_rows = atoms * count_b * 2
    grow = iota((gather_rows, count_b * spots), 0)
    gcol = iota((gather_rows, count_b * spots), 1)
    gather = one_hot(jnp.logical_and(
        gcol // pairs % 2 + 2 * (gcol // spots) == grow % (2 * count_b),
        gcol % pairs // per_atom == grow // (2 * count_b),
    ))
    picked = []
    for i in range(kinds):
        pick = one_hot(iota((ijs, width), 0) == i * kinds + iota((ijs, width), 1) % unit // block)
        picked.append(dot(gather, jnp.where(fits, dot(flat, pick), 0.0).astype(BF)))
    deep = kinds * count_b * 2
    hues = 2 * count_k
    stacks = []
    for atom in range(atoms):
        rows = jnp.concatenate([p[atom * 2 * count_b:(atom + 1) * 2 * count_b] for p in picked], axis=0)
        hue = iota((deep, width), 1) % hues
        stacks.append(jnp.concatenate([jnp.where(hue == h, rows, 0.0) for h in range(hues)], axis=0).astype(BF))

    crow = iota((unit, hues * deep), 0)
    ccol = iota((unit, hues * deep), 1)
    c_row, c_col = crow % 2, ccol // deep % 2
    part, b_col = ccol % 2, ccol % (2 * count_b) // 2
    fixed = jnp.logical_and(
        crow // block == ccol % deep // (2 * count_b), part == jnp.where(c_row == c_col, 0, 1)
    )
    signed = jnp.where(fixed, jnp.where(c_row < c_col, -1.0, 1.0), 0.0)
    b_want = b_col.astype(F32)
    pick_k = one_hot(iota((unit, count_k), 1) == iota((unit, count_k), 0) % (2 * count_k) // 2)
    same_pair = iota((unit, width), 0) % block // hues == iota((unit, width), 1) % block // hues
    nk = table_ref.shape[1]

    def select(first):
        table = table_ref[...].astype(F32).astype(BF)
        k2 = iota((nk, hues * deep), 1) // (2 * deep)
        want = one_hot(iota((nk, hues * deep), 0) == first + k2)
        index = dot(dot(pick_k, table).astype(BF), want)
        return jnp.where(index == b_want, signed, 0.0).astype(BF)

    def coefficients(sel, atom):
        return jnp.where(same_pair, dot(sel, stacks[atom]), 0.0).astype(BF)

    sides = {}
    for r in range(moms):
        sel = select(lax.rem(mom + r, moms) * count_k)
        count = moms - 1 if r > 0 else 1
        at = max(r - 1, 0) * side
        for atom in range(atoms):
            coef = coefficients(sel, atom)
            for d in range(2):
                src, dst = iota((width, count * side), 0), iota((width, count * side), 1)
                inside = jnp.logical_and(src >= d * side, src < (d + 1) * side)
                move = one_hot(jnp.logical_and(dst - at == src - d * side, inside))
                sides.setdefault((min(r, 1), d, atom), []).append(dot(coef, move))
    for (others, d, atom), pieces in sides.items():
        (coef_side if others else coef_own)[d, atom] = sum(pieces[1:], pieces[0]).astype(BF)

    tiles = q // tile

    def rotate(r, place, members=range(atoms)):
        for atom in members:
            found = []
            for p in range(per_atom):
                rows = jnp.concatenate(
                    [bufs[r][:, place * count_e + e, atom * per_atom + p].reshape(2 * count_k, q) for e in range(count_e)], axis=0
                )
                rows = jnp.concatenate([rows[:, t * tile:(t + 1) * tile] for t in range(tiles)], axis=0)
                found.append(dot(rows, right[neigh_ref[p, atom]]).reshape(tiles, count_e, 2 * count_k, kinds * tile))
            for j in range(kinds):
                for t in range(tiles):
                    both = jnp.concatenate([f[t, :, :, j * tile:(j + 1) * tile] for f in found], axis=1).astype(BF)
                    rots[atom][r, pl.ds(place * count_e, count_e), j * block:(j + 1) * block, t * tile:(t + 1) * tile] = both

    def term(coef, group, atom, d, e):
        window = jnp.concatenate(
            [rots[atom][r, e + count_e + (2 * d - 1) * shift_ref[w]] for r in group for w in range(freqs)], axis=0
        )
        return dot(coef[d, atom], window)

    rest = range(1, moms)

    def add(coef, group, d, fresh=False):
        for atom in range(atoms):
            for e in range(count_e):
                piece = term(coef, group, atom, d, e)
                sums[atom, e] = piece if fresh else sums[atom, e] + piece

    own.wait()
    rotate(0, 1)
    for k in range(turns):
        halo_copy(far, 0, k).wait_recv()
    rotate(0, 2 * far)
    add(coef_own, [0], far, True)
    for k in range(turns):
        for r in rest:
            mom_copy(r, k).wait_recv()
            if k < split:
                @pl.when(has_far)
                def _():
                    halo_copy(far, r, k).start()
        late = k + split
        if late < turns:
            @pl.when(has_far)
            def _():
                halo_copy(near, 0, late).wait_recv()
                for r in rest:
                    relay_copy(r, late).start()
        for r in rest:
            halo_copy(near, r, k).start()

    for r in rest:
        rotate(r, 1)

    @pl.when(has_far)
    def _():
        for k in range(split):
            halo_copy(near, 0, k).wait_recv()

    rotate(0, 2 * near)
    add(coef_own, [0], near)
    if moms > 1:
        for r in rest:
            for k in range(turns):
                halo_copy(far, r, k).wait_recv()
            rotate(r, 2 * far)
        add(coef_side, rest, far)

        @pl.when(has_far)
        def _():
            for r in rest:
                for k in range(turns):
                    halo_copy(near, r, k).wait_recv()

    def turn(atom):
        for r in rest:
            rotate(r, 2 * near, [atom])

    halves = {}

    def close(atom):
        rows = [[] for _ in range(kinds)]
        for e in range(count_e):
            total = sums[atom, e]
            if moms > 1:
                total = total + term(coef_side, rest, atom, near, e)
            total = total.astype(BF)
            for i in range(kinds):
                rows[i].append(total[i * block:(i + 1) * block])
        halves[atom] = [jnp.concatenate(row, axis=0) for row in rows]

    def finish(atom):
        result = dot(jnp.concatenate(halves.pop(atom), axis=1), left[atom])
        for e in range(count_e):
            for p in range(per_atom):
                for k in range(count_k):
                    at = e * block + (p * count_k + k) * 2
                    out_ref[k, e, atom * per_atom + p] = result[at:at + 2]

    steps = [turn, close, finish]
    for step in steps:
        for atom in range(atoms):
            step(atom)

    for k in range(turns):
        for r in range(moms):
            when_sent(r, k, lambda copy: copy.wait_send())
            if r > 0:
                mom_copy(r, k).wait_send()
                if k >= split:
                    @pl.when(has_far)
                    def _():
                        relay_copy(r, k).wait_send()


def shards(green, phonon, coupling, neighbours, momentum_table, shifts):
    moms, slabs = lax.axis_size("mom"), lax.axis_size("en")
    count_k, count_e, pairs = green.shape[:3]
    q = green.shape[4]
    kinds, atoms = coupling.shape[:2]
    ijs = phonon.shape[3]
    count_b = phonon.shape[0]
    spread = phonon.transpose(0, 1, 2, 4, 5, 3).reshape(count_b, -1, ijs)
    tile = 128
    block = pairs // atoms * count_k * 2
    unit = kinds * block
    side = shifts.shape[0] * unit
    dma = pltpu.SemaphoreType.DMA
    args = (neighbours.T, shifts, momentum_table, green, spread, coupling)
    return pl.pallas_call(
        functools.partial(kernel, moms, slabs),
        out_shape=pltpu.VMEM(green.shape, F32),
        in_specs=[pl.BlockSpec(memory_space=pltpu.HBM)] * len(args),
        out_specs=pl.BlockSpec(memory_space=pltpu.VMEM),
        scratch_shapes=[
            pltpu.SMEM(neighbours.T.shape, jnp.int32),
            pltpu.SMEM(shifts.shape, jnp.int32),
            pltpu.VMEM(momentum_table.shape, jnp.int32),
            pltpu.VMEM(spread.shape, BF),
            pltpu.VMEM(coupling.shape, BF),
            pltpu.VMEM((atoms, tile, kinds * tile), BF),
            pltpu.VMEM((atoms, kinds * q, q), BF),
            pltpu.VMEM((2, atoms, unit, side), BF),
            pltpu.VMEM((2, atoms, unit, max(moms - 1, 1) * side), BF),
            pltpu.VMEM((atoms, count_e, unit, q), F32),
            dma((5,)),
            dma,
            dma((moms, count_k)),
            dma((moms, count_k)),
            dma((2, moms, count_k)),
            dma((2, moms, count_k)),
            dma((moms, count_k)),
        ] + [pltpu.VMEM((count_k, 3 * count_e, pairs, 2, q), BF)] * moms
        + [pltpu.VMEM((moms, 3 * count_e, unit, q), BF)] * atoms,
        compiler_params=pltpu.CompilerParams(
            collective_id=0, has_side_effects=True, vmem_limit_bytes=48 * 1024 * 1024
        ),
    )(*[pltpu.with_memory_space_constraint(x, pltpu.HBM) for x in args])


def solution(mesh):
    return jax.shard_map(
        shards,
        mesh=mesh,
        in_specs=(P("mom", "en", None, None, None), P(), P(), P(), P("mom", None), P()),
        out_specs=P("mom", "en", None, None, None),
        check_vma=False,
    )
```
